32 devices in a mesh: order: 8 (over z, x), chan: 4 (over y, core).
Axes of the slice: x: 2, y: 2, z: 4, core: 2. Of those that a mesh axis runs over, the one named last changes fastest.
Arguments:
- cotangent: bfloat16 [248, 240, 1, 2, 1024], P('order', None, None, None, 'chan'), may hold values from -0.59765625 to 0.59765625
- stored_coefficients: bfloat16 [248, 240, 1, 2, 1024], P('order', None, None, None, 'chan'), may hold values from -0.29882812 to 0.29882812
- weights: bfloat16 [248, 1024, 1024], P('order', 'chan'), may hold values from -0.1875 to 0.1875
- order_table: int32 [248], replicated, may hold values from 0 to 240, as said below
- degree_table: int32 [248], replicated, may hold values from 0 to 240, as said below
Outputs:
- input_gradient: bfloat16 [248, 240, 1, 2, 1024], P('order', None, None, None, 'chan')
- mixing_gradient: bfloat16 [248, 1024, 1024], P('order', 'chan')
The draws below stay inside these ranges and needn't reach their ends.
Inputs may be any that keep to these rules, and one draw needn't show every extreme that they name: `order_table`: each order 0 to 239 stands in exactly one slot; every other slot holds 240, meaning empty. `degree_table`: each degree 0 to 239 stands in exactly one slot; every other slot holds 240, meaning empty.
All inputs are finite; a program needn't handle non-finite values.
Results may differ from the reference program's by a relative error of at most 0.008.
Values may be sent and summed in bfloat16 or wider, within the bound.
A program may use at most 192 MiB of HBM per device.

```python
import jax
import jax.numpy as jnp
from jax import lax

DEGREE_COUNT = 240
LATITUDE_COUNT = 240
CHANNEL_COUNT = 1024
BATCH_SAMPLES = 1
TOTAL_SLOTS = 248


def draw_order_table(key, part):
    permuted_values = jax.random.permutation(jax.random.fold_in(key, 101), TOTAL_SLOTS)
    return jnp.minimum(permuted_values, DEGREE_COUNT).astype(jnp.int32)


def draw_degree_table(key, part):
    permuted_values = jax.random.permutation(jax.random.fold_in(key, 202), TOTAL_SLOTS)
    return jnp.minimum(permuted_values, DEGREE_COUNT).astype(jnp.int32)


def levels(stream_key, extent, split, least, largest):
    def one(position, shards_of):
        draws = jax.random.uniform(jax.random.fold_in(jax.random.fold_in(stream_key, 6), position), (shards_of,), jnp.float32, least / len(split), largest / len(split))
        return jnp.repeat(jnp.exp(draws), extent[position] // shards_of).reshape((-1,) + (1,) * (len(extent) - position - 1))

    loudness = one(*split[0])
    for cut in split[1:]:
        loudness = loudness * one(*cut)
    return loudness


def noise(key, dims, deviation, bound, pieces=(), held_as=jnp.bfloat16):
    values = jax.random.normal(key, dims, jnp.float32) * deviation
    if len(pieces) > 0:
        values = levels(key, dims, pieces, -0.22, 0.18) * values
    return jnp.clip(values, min=-bound, max=bound).astype(held_as)


def setup_inputs(seed: int = 0) -> dict:
    keys = jax.random.split(jax.random.key(seed), 6)
    return {
        "cotangent": noise(keys[0], (TOTAL_SLOTS, LATITUDE_COUNT, BATCH_SAMPLES, 2, CHANNEL_COUNT), 0.1, 0.59765625, ((0, 8), (4, 4))),
        "stored_coefficients": noise(keys[1], (TOTAL_SLOTS, DEGREE_COUNT, BATCH_SAMPLES, 2, CHANNEL_COUNT), 0.05, 0.29882812, ((0, 8), (4, 4))),
        "weights": noise(keys[2], (TOTAL_SLOTS, CHANNEL_COUNT, CHANNEL_COUNT), CHANNEL_COUNT ** -0.5, 0.1875, ((0, 8), (1, 4))),
        "order_table": draw_order_table(jax.random.fold_in(keys[5], 71), 0),
        "degree_table": draw_degree_table(jax.random.fold_in(keys[5], 71), 0),
    }


def legendre_rows(orders, degree_range, latitude_count):
    order_real = orders.astype(jnp.float32)[:, None]
    angles = jnp.pi * (jnp.arange(latitude_count).astype(jnp.float32) + 0.5) / latitude_count
    cosine = jnp.cos(angles)[None, :]
    sine = jnp.sin(angles)[None, :]
    counter = jnp.arange(1, degree_range + 1).astype(jnp.float32)
    factors = jnp.log((2.0 * counter - 1.0) / (2.0 * counter))
    below = (counter[None, :] <= order_real).astype(jnp.float32)
    log_start = 0.5 * (jnp.log((2.0 * order_real + 1.0) / (4.0 * jnp.pi)) + lax.optimization_barrier(jnp.sum(below * factors[None, :], axis=1, keepdims=True)))
    parity = 1.0 - 2.0 * (orders % 2).astype(jnp.float32)[:, None]
    start = parity * jnp.exp(log_start + order_real * jnp.log(sine))

    def advance(carry, degree):
        latest, before = carry
        level = degree.astype(jnp.float32)
        upper = jnp.sqrt(jnp.maximum(4.0 * level * level - 1.0, 0.0) / jnp.maximum(level * level - order_real * order_real, 1.0))
        lower = jnp.sqrt(jnp.maximum((level - 1.0) * (level - 1.0) - order_real * order_real, 0.0) / jnp.maximum(4.0 * (level - 1.0) * (level - 1.0) - 1.0, 1.0))
        grown = upper * (cosine * latest - lower * before)
        fresh = jnp.where(level == order_real, start, jnp.where(level > order_real, grown, jnp.zeros_like(grown)))
        return ((fresh, latest), fresh)
    zeros = jnp.zeros((orders.shape[0], latitude_count), jnp.float32)
    unused_result, stacked = lax.scan(advance, (zeros, zeros), jnp.arange(degree_range).astype(jnp.int32))
    return jnp.transpose(stacked, (1, 0, 2))

def quadrature(latitude_count):
    angles = jnp.pi * (jnp.arange(latitude_count).astype(jnp.float32) + 0.5) / latitude_count
    return jnp.pi / latitude_count * jnp.sin(angles)

def reference(cotangent, stored_coefficients, weights, order_table, degree_table):
    slot_count, latitude_count, batch_size, unused_result, slot_width = cotangent.shape
    degree_range = stored_coefficients.shape[1]
    feature_count = batch_size * 2 * slot_width
    table = legendre_rows(order_table, degree_range, latitude_count)
    table_halfprecision = table.astype(jnp.bfloat16)
    flat_cotangent = cotangent.reshape(slot_count, latitude_count, feature_count)

    def synth_adjoint(items):
        table_one, cot_one = items
        return jnp.dot(table_one.astype(jnp.float32), cot_one.astype(jnp.float32), preferred_element_type=jnp.float32).astype(jnp.bfloat16)
    adjoint = lax.map(synth_adjoint, (table_halfprecision, flat_cotangent))
    active_mask = jnp.arange(degree_range).astype(jnp.int32)[None, :] >= order_table[:, None]
    masked_values = stored_coefficients.reshape(slot_count, degree_range, feature_count) * active_mask[:, :, None].astype(jnp.bfloat16)
    clipped = jnp.minimum(degree_table, degree_range - 1).astype(jnp.int32)
    valid_degree = degree_table < degree_range

    def per_degree(items):
        degree_one, valid_one, weight_one = items
        left_row_block = lax.dynamic_index_in_dim(masked_values, degree_one, 1, keepdims=False)
        right_row_block = lax.dynamic_index_in_dim(adjoint, degree_one, 1, keepdims=False)
        left_flattened = left_row_block.reshape(slot_count * batch_size * 2, slot_width).astype(jnp.float32)
        right_flattened = right_row_block.reshape(slot_count * batch_size * 2, slot_width).astype(jnp.float32)
        weight_gradient = jnp.dot(left_flattened.T, right_flattened, preferred_element_type=jnp.float32)
        weight_gradient = jnp.where(valid_one, weight_gradient, jnp.zeros_like(weight_gradient)).astype(jnp.bfloat16)
        coefficient_gradient = jnp.dot(right_flattened, weight_one.astype(jnp.float32).T, preferred_element_type=jnp.float32)
        coefficient_gradient = jnp.where(valid_one, coefficient_gradient, jnp.zeros_like(coefficient_gradient)).astype(jnp.bfloat16)
        return (weight_gradient, coefficient_gradient.reshape(slot_count, feature_count))
    mixing_gradient, grad_coeff = lax.map(per_degree, (clipped, valid_degree, weights))
    quad = quadrature(latitude_count)

    def order_values(items):
        table_one, index_one = items
        picked = jnp.take(table_one, clipped, axis=0) * valid_degree[:, None].astype(jnp.bfloat16)
        grads = lax.dynamic_index_in_dim(grad_coeff, index_one, 1, keepdims=False)
        summed = jnp.dot(picked.astype(jnp.float32).T, grads.astype(jnp.float32), preferred_element_type=jnp.float32)
        return (summed * quad[:, None]).astype(jnp.bfloat16)
    input_gradient = lax.map(order_values, (table_halfprecision, jnp.arange(slot_count).astype(jnp.int32)))
    return (input_gradient.reshape(slot_count, latitude_count, batch_size, 2, slot_width), mixing_gradient)
```

```python
import functools

import jax
import jax.numpy as jnp
from jax import lax
from jax.experimental import pallas as pl
from jax.experimental.pallas import tpu as pltpu
from jax.sharding import PartitionSpec as P

CHUNKS = 2
LANES = 128


def recurrence_kernel(unroll, where_ref, upper_ref, lower_ref, order_ref, cosine_ref, start_ref, out_ref):
    degree_range = upper_ref.shape[0]
    latitude_count = out_ref.shape[2]
    pieces = [(lo, min(lo + LANES, latitude_count)) for lo in range(0, latitude_count, LANES)]
    out_ref[...] = jnp.zeros_like(out_ref)
    order = order_ref[...]
    cosine = [cosine_ref[:, lo:hi] for lo, hi in pieces]
    start = [start_ref[:, lo:hi] for lo, hi in pieces]

    def body(step, carry):
        latest, before = carry
        for inner in range(unroll):
            level = step * unroll + inner
            row = where_ref[level]
            upper = upper_ref[level]
            lower = lower_ref[level]
            begins = order == level
            fresh = []
            for i, (lo, hi) in enumerate(pieces):
                width = hi - lo
                grown = upper[:, :width] * (cosine[i] * latest[i] - lower[:, :width] * before[i])
                value = jnp.where(begins[:, :width], start[i], grown)
                out_ref[row, :, lo:hi] = value.astype(jnp.bfloat16)
                fresh.append(value)
            latest, before = fresh, latest
        return latest, before

    zeros = [jnp.zeros_like(c) for c in cosine]
    lax.fori_loop(0, degree_range // unroll, body, (zeros, zeros))


def picked_legendre(orders, degree_table, degree_range, latitude_count):
    slots = orders.shape[0]
    total = degree_table.shape[0]
    order_real = orders.astype(jnp.float32)[:, None]
    angles = jnp.pi * (jnp.arange(latitude_count).astype(jnp.float32) + 0.5) / latitude_count
    cosine = jnp.cos(angles)[None, :]
    sine = jnp.sin(angles)[None, :]
    counter = jnp.arange(1, degree_range + 1).astype(jnp.float32)
    factors = jnp.log((2.0 * counter - 1.0) / (2.0 * counter))
    below = (counter[None, :] <= order_real).astype(jnp.float32)
    log_start = 0.5 * (
        jnp.log((2.0 * order_real + 1.0) / (4.0 * jnp.pi))
        + jnp.sum(below * factors[None, :], axis=1, keepdims=True)
    )
    parity = 1.0 - 2.0 * (orders % 2).astype(jnp.float32)[:, None]
    start = parity * jnp.exp(log_start + order_real * jnp.log(sine))

    level = jnp.arange(degree_range).astype(jnp.float32)[:, None, None]
    order_wide = jnp.broadcast_to(order_real[None], (1, slots, LANES))
    upper = jnp.sqrt(
        jnp.maximum(4.0 * level * level - 1.0, 0.0)
        / jnp.maximum(level * level - order_wide * order_wide, 1.0)
    )
    lower = jnp.sqrt(
        jnp.maximum((level - 1.0) * (level - 1.0) - order_wide * order_wide, 0.0)
        / jnp.maximum(4.0 * (level - 1.0) * (level - 1.0) - 1.0, 1.0)
    )
    places = jnp.arange(total).astype(jnp.int32)
    degrees = jnp.arange(degree_range).astype(jnp.int32)
    where = jnp.sum(
        jnp.where(degree_table[None, :] == degrees[:, None], places[None, :], 0), axis=1
    )
    where = jnp.minimum(where, total - 1).astype(jnp.int32)
    unroll = next(u for u in (8, 6, 5, 4, 3, 2, 1) if degree_range % u == 0)
    vmem = pl.BlockSpec(memory_space=pltpu.VMEM)
    return pl.pallas_call(
        functools.partial(recurrence_kernel, unroll),
        out_shape=jax.ShapeDtypeStruct((total, slots, latitude_count), jnp.bfloat16),
        in_specs=[pl.BlockSpec(memory_space=pltpu.SMEM)] + [vmem] * 5,
        out_specs=vmem,
        cost_estimate=pl.CostEstimate(
            flops=6 * degree_range * slots * latitude_count,
            bytes_accessed=24 * 1024 * 1024,
            transcendentals=0,
        ),
        name="legendre",
    )(
        where,
        upper,
        lower,
        jnp.broadcast_to(orders[:, None], (slots, LANES)),
        jnp.broadcast_to(cosine, (slots, latitude_count)),
        start,
    )


def quadrature(latitude_count):
    angles = jnp.pi * (jnp.arange(latitude_count).astype(jnp.float32) + 0.5) / latitude_count
    return jnp.pi / latitude_count * jnp.sin(angles)


def per_device(cotangent, stored_coefficients, weights, order_table, degree_table):
    slots, latitude_count, batch_size, parts, width = cotangent.shape
    degree_range = stored_coefficients.shape[1]
    rows = batch_size * parts
    peers = lax.axis_size("order")
    position = lax.axis_index("order")
    mine = lax.dynamic_slice_in_dim(order_table, position * slots, slots)
    table = picked_legendre(mine, degree_table, degree_range, latitude_count)
    table = table.reshape(peers, slots, slots, latitude_count)
    cot = cotangent.reshape(slots, latitude_count, rows, width)
    stored = stored_coefficients.reshape(slots, degree_range, rows, width)
    degrees = jnp.arange(degree_range).astype(jnp.int32)
    pick = (degree_table[:, None, None] == degrees[None, None, :]) & (
        degrees[None, None, :] >= mine[None, :, None]
    )
    pick = pick.astype(jnp.bfloat16).reshape(peers, slots, slots, degree_range)

    chunks = min(CHUNKS, slots)
    edges = [slots * i // chunks for i in range(chunks + 1)]
    spans = list(zip(edges[:-1], edges[1:]))

    def exchange(value):
        return lax.all_to_all(value, "order", split_axis=0, concat_axis=0, tiled=True)

    def project(matrix, source, lo, hi):
        return jnp.einsum(
            "tksj,sjrc->tkrsc", matrix[:, lo:hi], source, preferred_element_type=jnp.float32
        ).astype(jnp.bfloat16)

    saved, adjoint, gathered = [], [], []
    for lo, hi in spans:
        adjoint.append(exchange(project(table, cot, lo, hi)))
        gathered.append(lax.all_gather(adjoint[-1], "chan", axis=4, tiled=True))
    for lo, hi in spans:
        saved.append(exchange(project(pick, stored, lo, hi)))
    returned = []
    for i, (lo, hi) in enumerate(spans):
        coefficient = jnp.einsum(
            "nkrsd,kcd->nkrsc", gathered[i], weights[lo:hi], preferred_element_type=jnp.float32
        ).astype(jnp.bfloat16)
        returned.append(exchange(coefficient))
    mixing = []
    for i in range(chunks):
        mixing.append(
            jnp.einsum(
                "nkrsc,nkrsd->kcd", saved[i], gathered[i], preferred_element_type=jnp.float32
            ).astype(jnp.bfloat16)
        )
    mixing_gradient = jnp.concatenate(mixing, axis=0)
    back = jnp.concatenate(returned, axis=1)
    summed = jnp.einsum("tksj,tkrsc->sjrc", table, back, preferred_element_type=jnp.float32)
    quad = quadrature(latitude_count)
    input_gradient = (summed * quad[None, :, None, None]).astype(jnp.bfloat16)
    return input_gradient.reshape(cotangent.shape), mixing_gradient


def solution(mesh):
    return jax.shard_map(
        per_device,
        mesh=mesh,
        in_specs=(
            P("order", None, None, None, "chan"),
            P("order", None, None, None, "chan"),
            P("order", "chan", None),
            P(),
            P(),
        ),
        out_specs=(P("order", None, None, None, "chan"), P("order", "chan", None)),
        check_vma=False,
    )
```

```python
import functools

import jax
import jax.numpy as jnp
from jax import lax
from jax.experimental import pallas as pl
from jax.experimental.pallas import tpu as pltpu
from jax.sharding import PartitionSpec as P

SPREADS = 3.5
LANES = 128


def recurrence_kernel(unroll, where_ref, upper_ref, lower_ref, order_ref, cosine_ref, start_ref, out_ref):
    degree_range = upper_ref.shape[0]
    latitude_count = out_ref.shape[2]
    pieces = [(lo, min(lo + LANES, latitude_count)) for lo in range(0, latitude_count, LANES)]
    out_ref[...] = jnp.zeros_like(out_ref)
    order = order_ref[...]
    cosine = [cosine_ref[:, lo:hi] for lo, hi in pieces]
    start = [start_ref[:, lo:hi] for lo, hi in pieces]

    def body(step, carry):
        latest, before = carry
        for inner in range(unroll):
            level = step * unroll + inner
            row = where_ref[level]
            upper = upper_ref[level]
            lower = lower_ref[level]
            begins = order == level
            fresh = []
            for i, (lo, hi) in enumerate(pieces):
                width = hi - lo
                grown = upper[:, :width] * (cosine[i] * latest[i] - lower[:, :width] * before[i])
                value = jnp.where(begins[:, :width], start[i], grown)
                out_ref[row, :, lo:hi] = value.astype(jnp.bfloat16)
                fresh.append(value)
            latest, before = fresh, latest
        return latest, before

    zeros = [jnp.zeros_like(c) for c in cosine]
    lax.fori_loop(0, degree_range // unroll, body, (zeros, zeros))


def picked_legendre(orders, degree_table, degree_range, latitude_count):
    slots = orders.shape[0]
    total = degree_table.shape[0]
    order_real = orders.astype(jnp.float32)[:, None]
    angles = jnp.pi * (jnp.arange(latitude_count).astype(jnp.float32) + 0.5) / latitude_count
    cosine = jnp.cos(angles)[None, :]
    sine = jnp.sin(angles)[None, :]
    counter = jnp.arange(1, degree_range + 1).astype(jnp.float32)
    factors = jnp.log((2.0 * counter - 1.0) / (2.0 * counter))
    below = (counter[None, :] <= order_real).astype(jnp.float32)
    log_start = 0.5 * (
        jnp.log((2.0 * order_real + 1.0) / (4.0 * jnp.pi))
        + jnp.sum(below * factors[None, :], axis=1, keepdims=True)
    )
    parity = 1.0 - 2.0 * (orders % 2).astype(jnp.float32)[:, None]
    start = parity * jnp.exp(log_start + order_real * jnp.log(sine))

    level = jnp.arange(degree_range).astype(jnp.float32)[:, None, None]
    order_wide = jnp.broadcast_to(order_real[None], (1, slots, LANES))
    upper = jnp.sqrt(
        jnp.maximum(4.0 * level * level - 1.0, 0.0)
        / jnp.maximum(level * level - order_wide * order_wide, 1.0)
    )
    lower = jnp.sqrt(
        jnp.maximum((level - 1.0) * (level - 1.0) - order_wide * order_wide, 0.0)
        / jnp.maximum(4.0 * (level - 1.0) * (level - 1.0) - 1.0, 1.0)
    )
    places = jnp.arange(total).astype(jnp.int32)
    degrees = jnp.arange(degree_range).astype(jnp.int32)
    where = jnp.sum(
        jnp.where(degree_table[None, :] == degrees[:, None], places[None, :], 0), axis=1
    )
    where = jnp.minimum(where, total - 1).astype(jnp.int32)
    unroll = next(u for u in (8, 6, 5, 4, 3, 2, 1) if degree_range % u == 0)
    vmem = pl.BlockSpec(memory_space=pltpu.VMEM)
    return pl.pallas_call(
        functools.partial(recurrence_kernel, unroll),
        out_shape=jax.ShapeDtypeStruct((total, slots, latitude_count), jnp.bfloat16),
        in_specs=[pl.BlockSpec(memory_space=pltpu.SMEM)] + [vmem] * 5,
        out_specs=vmem,
        cost_estimate=pl.CostEstimate(
            flops=6 * degree_range * slots * latitude_count,
            bytes_accessed=24 * 1024 * 1024,
            transcendentals=0,
        ),
        name="legendre",
    )(
        where,
        upper,
        lower,
        jnp.broadcast_to(orders[:, None], (slots, LANES)),
        jnp.broadcast_to(cosine, (slots, latitude_count)),
        start,
    )


def quadrature(latitude_count):
    angles = jnp.pi * (jnp.arange(latitude_count).astype(jnp.float32) + 0.5) / latitude_count
    return jnp.pi / latitude_count * jnp.sin(angles)


def dense_exchange(peers, slots):
    def exchange(value):
        moved = lax.all_to_all(
            value.reshape(peers, slots, slots, value.shape[-1]),
            "order",
            split_axis=0,
            concat_axis=0,
            tiled=True,
        )
        return moved

    return exchange, exchange


def packed_exchange(peers, slots, capacity, leave, arrive):
    place = jnp.arange(capacity).astype(jnp.int32)[None, :, None, None]
    leave_matrix = (leave[:, None] == place).astype(jnp.bfloat16)
    arrive_matrix = (arrive[:, None] == place).astype(jnp.bfloat16)

    def route(value, packer, unpacker):
        packed = jnp.einsum(
            "tpks,tksc->tpc", packer, value, preferred_element_type=jnp.float32
        ).astype(jnp.bfloat16)
        moved = lax.all_to_all(packed, "order", split_axis=0, concat_axis=0, tiled=True)
        return jnp.einsum(
            "tpks,tpc->tksc", unpacker, moved, preferred_element_type=jnp.float32
        ).astype(jnp.bfloat16)

    return (
        lambda value: route(value, leave_matrix, arrive_matrix),
        lambda value: route(value, arrive_matrix, leave_matrix),
    )


def layer(send, back, cotangent, stored_coefficients, weights, table, pick):
    slots, latitude_count, batch_size, parts, width = cotangent.shape
    degree_range = stored_coefficients.shape[1]
    rows = batch_size * parts
    cot = cotangent.reshape(slots, latitude_count, rows, width)
    stored = stored_coefficients.reshape(slots, degree_range, rows, width)

    def project(matrix, source):
        return jnp.einsum(
            "tksj,sjc->tksc", matrix, source, preferred_element_type=jnp.float32
        ).astype(jnp.bfloat16)

    gathered, saved, mixing, outputs = [], [], [], []
    for r in range(rows):
        adjoint = send(project(table, cot[:, :, r]))
        gathered.append(lax.all_gather(adjoint, "chan", axis=3, tiled=True))
    for r in range(rows):
        saved.append(send(project(pick, stored[:, :, r])))
    quad = quadrature(latitude_count)
    for r in range(rows):
        coefficient = jnp.einsum(
            "nksd,kcd->nksc", gathered[r], weights, preferred_element_type=jnp.float32
        ).astype(jnp.bfloat16)
        summed = jnp.einsum(
            "tksj,tksc->sjc", table, back(coefficient), preferred_element_type=jnp.float32
        )
        outputs.append((summed * quad[None, :, None]).astype(jnp.bfloat16))
    for r in range(rows):
        mixing.append(
            jnp.einsum("nksc,nksd->kcd", saved[r], gathered[r], preferred_element_type=jnp.float32)
        )
    mixing_gradient = sum(mixing[1:], mixing[0]).astype(jnp.bfloat16)
    return jnp.stack(outputs, axis=2).reshape(cotangent.shape), mixing_gradient


def per_device(cotangent, stored_coefficients, weights, order_table, degree_table):
    slots, latitude_count = cotangent.shape[:2]
    degree_range = stored_coefficients.shape[1]
    peers = lax.axis_size("order")
    position = lax.axis_index("order")
    mine = lax.dynamic_slice_in_dim(order_table, position * slots, slots)
    owned = lax.dynamic_slice_in_dim(degree_table, position * slots, slots)
    table = picked_legendre(mine, degree_table, degree_range, latitude_count)
    table = table.reshape(peers, slots, slots, latitude_count)
    degrees = jnp.arange(degree_range).astype(jnp.int32)
    pick = (degree_table[:, None, None] == degrees[None, None, :]) & (
        degrees[None, None, :] >= mine[None, :, None]
    )
    pick = pick.astype(jnp.bfloat16).reshape(peers, slots, slots, degree_range)
    operands = (cotangent, stored_coefficients, weights, table, pick)

    full = slots * slots
    live = degree_range * (degree_range + 1) / 2 / (peers * slots) ** 2
    spread = (full * (2 * slots + 1) / 12) ** 0.5
    capacity = -(-int(live * full + SPREADS * spread) // 16) * 16
    dense = functools.partial(layer, *dense_exchange(peers, slots))
    if capacity > 0.85 * full:
        return dense(*operands)

    def places(orders, degree_rows):
        valid = (degree_rows >= orders) & (degree_rows < degree_range)
        flags = valid.reshape(-1, full).astype(jnp.bfloat16)
        index = jnp.arange(full)
        before = (index[:, None] < index[None, :]).astype(jnp.bfloat16)
        rank = jnp.dot(flags, before, preferred_element_type=jnp.float32).astype(jnp.int32)
        return jnp.where(valid, rank.reshape(valid.shape), -1)

    leave = places(mine[None, None, :], degree_table.reshape(peers, slots)[:, :, None])
    arrive = places(order_table.reshape(peers, slots)[:, None, :], owned[None, :, None])
    order_rows = order_table.reshape(peers, 1, slots, 1)
    degree_rows = degree_table.reshape(1, peers, 1, slots)
    counts = jnp.sum(
        ((degree_rows >= order_rows) & (degree_rows < degree_range)).astype(jnp.int32), axis=(2, 3)
    )
    fits = jnp.max(counts) <= capacity
    packed = functools.partial(layer, *packed_exchange(peers, slots, capacity, leave, arrive))
    return lax.cond(fits, packed, dense, *operands)


def solution(mesh):
    return jax.shard_map(
        per_device,
        mesh=mesh,
        in_specs=(
            P("order", None, None, None, "chan"),
            P("order", None, None, None, "chan"),
            P("order", "chan", None),
            P(),
            P(),
        ),
        out_specs=(P("order", None, None, None, "chan"), P("order", "chan", None)),
        check_vma=False,
    )
```

```python
import functools

import jax
import jax.numpy as jnp
from jax import lax
from jax.experimental import pallas as pl
from jax.experimental.pallas import tpu as pltpu
from jax.sharding import PartitionSpec as P


SPREADS = 3.5
LANES = 128


def recurrence_kernel(unroll, where_ref, upper_ref, lower_ref, order_ref, cosine_ref, start_ref, out_ref):
    degree_range = upper_ref.shape[0]
    latitude_count = out_ref.shape[2]
    pieces = [(lo, min(lo + LANES, latitude_count)) for lo in range(0, latitude_count, LANES)]
    out_ref[...] = jnp.zeros_like(out_ref)
    order = order_ref[...]
    cosine = [cosine_ref[:, lo:hi] for lo, hi in pieces]
    start = [start_ref[:, lo:hi] for lo, hi in pieces]

    def body(step, carry):
        latest, before = carry
        for inner in range(unroll):
            level = step * unroll + inner
            row = where_ref[level]
            upper = upper_ref[level]
            lower = lower_ref[level]
            begins = order == level
            fresh = []
            for i, (lo, hi) in enumerate(pieces):
                width = hi - lo
                grown = upper[:, :width] * (cosine[i] * latest[i] - lower[:, :width] * before[i])
                value = jnp.where(begins[:, :width], start[i], grown)
                out_ref[row, :, lo:hi] = value.astype(jnp.bfloat16)
                fresh.append(value)
            latest, before = fresh, latest
        return latest, before

    zeros = [jnp.zeros_like(c) for c in cosine]
    lax.fori_loop(0, degree_range // unroll, body, (zeros, zeros))


def picked_legendre(orders, degree_table, degree_range, latitude_count):
    slots = orders.shape[0]
    total = degree_table.shape[0]
    order_real = orders.astype(jnp.float32)[:, None]
    angles = jnp.pi * (jnp.arange(latitude_count).astype(jnp.float32) + 0.5) / latitude_count
    cosine = jnp.cos(angles)[None, :]
    sine = jnp.sin(angles)[None, :]
    counter = jnp.arange(1, degree_range + 1).astype(jnp.float32)
    factors = jnp.log((2.0 * counter - 1.0) / (2.0 * counter))
    below = (counter[None, :] <= order_real).astype(jnp.float32)
    log_start = 0.5 * (
        jnp.log((2.0 * order_real + 1.0) / (4.0 * jnp.pi))
        + jnp.sum(below * factors[None, :], axis=1, keepdims=True)
    )
    parity = 1.0 - 2.0 * (orders % 2).astype(jnp.float32)[:, None]
    start = parity * jnp.exp(log_start + order_real * jnp.log(sine))

    level = jnp.arange(degree_range).astype(jnp.float32)[:, None]
    order_wide = order_real[:, 0][None, :]
    upper = jnp.sqrt(
        jnp.maximum(4.0 * level * level - 1.0, 0.0)
        / jnp.maximum(level * level - order_wide * order_wide, 1.0)
    )
    lower = jnp.sqrt(
        jnp.maximum((level - 1.0) * (level - 1.0) - order_wide * order_wide, 0.0)
        / jnp.maximum(4.0 * (level - 1.0) * (level - 1.0) - 1.0, 1.0)
    )
    upper, lower = (
        jnp.broadcast_to(lax.optimization_barrier(part)[:, :, None], part.shape + (LANES,))
        for part in (upper, lower)
    )
    places = jnp.arange(total).astype(jnp.int32)
    degrees = jnp.arange(degree_range).astype(jnp.int32)
    where = jnp.sum(
        jnp.where(degree_table[None, :] == degrees[:, None], places[None, :], 0), axis=1
    )
    where = jnp.minimum(where, total - 1).astype(jnp.int32)
    unroll = next(u for u in (8, 6, 5, 4, 3, 2, 1) if degree_range % u == 0)
    vmem = pl.BlockSpec(memory_space=pltpu.VMEM)
    return pl.pallas_call(
        functools.partial(recurrence_kernel, unroll),
        out_shape=jax.ShapeDtypeStruct((total, slots, latitude_count), jnp.bfloat16),
        in_specs=[pl.BlockSpec(memory_space=pltpu.SMEM)] + [vmem] * 5,
        out_specs=vmem,
        cost_estimate=pl.CostEstimate(
            flops=6 * degree_range * slots * latitude_count,
            bytes_accessed=24 * 1024 * 1024,
            transcendentals=0,
        ),
        name="legendre",
    )(
        where,
        upper,
        lower,
        jnp.broadcast_to(orders[:, None], (slots, LANES)),
        jnp.broadcast_to(cosine, (slots, latitude_count)),
        start,
    )


def quadrature(latitude_count):
    angles = jnp.pi * (jnp.arange(latitude_count).astype(jnp.float32) + 0.5) / latitude_count
    return jnp.pi / latitude_count * jnp.sin(angles)


def dense_exchange():
    def exchange(value):
        return lax.all_to_all(value, "order", split_axis=0, concat_axis=0, tiled=True)

    return exchange, exchange


def packed_exchange(capacity, leave, arrive):
    place = jnp.arange(capacity).astype(jnp.int32)[None, :, None, None]
    leave_matrix = (leave[:, None] == place).astype(jnp.bfloat16)
    arrive_matrix = (arrive[:, None] == place).astype(jnp.bfloat16)

    def route(value, packer, unpacker):
        packed = jnp.einsum(
            "tpks,tksc->tpc", packer, value, preferred_element_type=jnp.float32
        ).astype(jnp.bfloat16)
        moved = lax.all_to_all(packed, "order", split_axis=0, concat_axis=0, tiled=True)
        return jnp.einsum(
            "tpks,tpc->tksc", unpacker, moved, preferred_element_type=jnp.float32
        ).astype(jnp.bfloat16)

    return (
        lambda value: route(value, leave_matrix, arrive_matrix),
        lambda value: route(value, arrive_matrix, leave_matrix),
    )


def layer(exchanges, cotangent, stored_coefficients, weights, table, mine, degree_table, *ranks):
    return layer_body(
        exchanges(*ranks), cotangent, stored_coefficients, weights, table, mine, degree_table
    )


def layer_body(exchanges, cotangent, stored_coefficients, weights, table, mine, degree_table):
    send, back = exchanges
    slots, latitude_count, batch_size, parts, width = cotangent.shape
    degree_range = stored_coefficients.shape[1]
    rows = batch_size * parts
    cot = cotangent.reshape(slots, latitude_count, rows, width)
    stored = stored_coefficients.reshape(slots, degree_range, rows, width)
    degrees = jnp.arange(degree_range).astype(jnp.int32)
    pick = (degree_table[:, None, None] == degrees[None, None, :]) & (
        degrees[None, None, :] >= mine[None, :, None]
    )
    pick = pick.astype(jnp.bfloat16).reshape(table.shape[:3] + (degree_range,))

    def project(matrix, source):
        return jnp.einsum(
            "tksj,sjc->tksc", matrix, source, preferred_element_type=jnp.float32
        ).astype(jnp.bfloat16)

    gathered, saved, mixing, outputs = [], [], [], []
    for r in range(rows):
        adjoint = send(project(table, cot[:, :, r]))
        gathered.append(lax.all_gather(adjoint, "chan", axis=3, tiled=True))
    for r in range(rows):
        saved.append(send(project(pick, stored[:, :, r])))
    quad = quadrature(latitude_count)
    for r in range(rows):
        coefficient = jnp.einsum(
            "nksd,kcd->nksc", gathered[r], weights, preferred_element_type=jnp.float32
        ).astype(jnp.bfloat16)
        summed = jnp.einsum(
            "tksj,tksc->sjc", table, back(coefficient), preferred_element_type=jnp.float32
        )
        outputs.append((summed * quad[None, :, None]).astype(jnp.bfloat16))
    for r in range(rows):
        mixing.append(
            jnp.einsum("nksc,nksd->kcd", saved[r], gathered[r], preferred_element_type=jnp.float32)
        )
    mixing_gradient = sum(mixing[1:], mixing[0]).astype(jnp.bfloat16)
    return jnp.stack(outputs, axis=2).reshape(cotangent.shape), mixing_gradient


def per_device(cotangent, stored_coefficients, weights, order_table, degree_table):
    slots, latitude_count = cotangent.shape[:2]
    degree_range = stored_coefficients.shape[1]
    peers = lax.axis_size("order")
    position = lax.axis_index("order")
    mine = lax.dynamic_slice_in_dim(order_table, position * slots, slots)
    owned = lax.dynamic_slice_in_dim(degree_table, position * slots, slots)
    table = picked_legendre(mine, degree_table, degree_range, latitude_count)
    table = table.reshape(peers, slots, slots, latitude_count)
    operands = (cotangent, stored_coefficients, weights, table, mine, degree_table)

    full = slots * slots
    live = degree_range * (degree_range + 1) / 2 / (peers * slots) ** 2
    spread = (full * (2 * slots + 1) / 12) ** 0.5
    capacity = -(-int(live * full + SPREADS * spread) // 16) * 16
    dense = functools.partial(layer, lambda *ranks: dense_exchange())
    if capacity > 0.85 * full:
        return dense(*operands)

    def places(orders, degree_rows):
        valid = (degree_rows >= orders) & (degree_rows < degree_range)
        flags = valid.reshape(-1, full).astype(jnp.bfloat16)
        index = jnp.arange(full)
        before = (index[:, None] < index[None, :]).astype(jnp.bfloat16)
        rank = jnp.dot(flags, before, preferred_element_type=jnp.float32).astype(jnp.int32)
        return jnp.where(valid, rank.reshape(valid.shape), -1)

    leave = places(mine[None, None, :], degree_table.reshape(peers, slots)[:, :, None])
    arrive = places(order_table.reshape(peers, slots)[:, None, :], owned[None, :, None])
    order_rows = order_table.reshape(peers, 1, slots, 1)
    degree_rows = degree_table.reshape(1, peers, 1, slots)
    counts = jnp.sum(
        ((degree_rows >= order_rows) & (degree_rows < degree_range)).astype(jnp.int32), axis=(2, 3)
    )
    fits = jnp.max(counts) <= capacity
    packed = functools.partial(layer, functools.partial(packed_exchange, capacity))
    return lax.cond(fits, packed, dense, *operands, leave, arrive)


def solution(mesh):
    return jax.shard_map(
        per_device,
        mesh=mesh,
        in_specs=(
            P("order", None, None, None, "chan"),
            P("order", None, None, None, "chan"),
            P("order", "chan", None),
            P(),
            P(),
        ),
        out_specs=(P("order", None, None, None, "chan"), P("order", "chan", None)),
        check_vma=False,
    )
```

```python
import functools

import jax
import jax.numpy as jnp
from jax import lax
from jax.experimental import pallas as pl
from jax.experimental.pallas import tpu as pltpu
from jax.sharding import PartitionSpec as P


SPREADS = 3.0
LANES = 128


def recurrence_kernel(unroll, where_ref, upper_ref, lower_ref, order_ref, cosine_ref, start_ref, out_ref):
    degree_range = upper_ref.shape[0]
    latitude_count = out_ref.shape[2]
    pieces = [(lo, min(lo + LANES, latitude_count)) for lo in range(0, latitude_count, LANES)]
    out_ref[...] = jnp.zeros_like(out_ref)
    order = order_ref[...]
    cosine = [cosine_ref[:, lo:hi] for lo, hi in pieces]
    start = [start_ref[:, lo:hi] for lo, hi in pieces]

    def body(step, carry):
        latest, before = carry
        for inner in range(unroll):
            level = step * unroll + inner
            row = where_ref[level]
            upper = upper_ref[level]
            lower = lower_ref[level]
            begins = order == level
            fresh = []
            for i, (lo, hi) in enumerate(pieces):
                width = hi - lo
                grown = upper[:, :width] * (cosine[i] * latest[i] - lower[:, :width] * before[i])
                value = jnp.where(begins[:, :width], start[i], grown)
                out_ref[row, :, lo:hi] = value.astype(jnp.bfloat16)
                fresh.append(value)
            latest, before = fresh, latest
        return latest, before

    zeros = [jnp.zeros_like(c) for c in cosine]
    lax.fori_loop(0, degree_range // unroll, body, (zeros, zeros))


def picked_legendre(orders, degree_table, degree_range, latitude_count):
    slots = orders.shape[0]
    total = degree_table.shape[0]
    order_real = orders.astype(jnp.float32)[:, None]
    angles = jnp.pi * (jnp.arange(latitude_count).astype(jnp.float32) + 0.5) / latitude_count
    cosine = jnp.cos(angles)[None, :]
    sine = jnp.sin(angles)[None, :]
    counter = jnp.arange(1, degree_range + 1).astype(jnp.float32)
    factors = jnp.log((2.0 * counter - 1.0) / (2.0 * counter))
    below = (counter[None, :] <= order_real).astype(jnp.float32)
    log_start = 0.5 * (
        jnp.log((2.0 * order_real + 1.0) / (4.0 * jnp.pi))
        + jnp.sum(below * factors[None, :], axis=1, keepdims=True)
    )
    parity = 1.0 - 2.0 * (orders % 2).astype(jnp.float32)[:, None]
    start = parity * jnp.exp(log_start + order_real * jnp.log(sine))

    level = jnp.arange(degree_range).astype(jnp.float32)[:, None]
    order_wide = order_real[:, 0][None, :]
    upper = jnp.sqrt(
        jnp.maximum(4.0 * level * level - 1.0, 0.0)
        / jnp.maximum(level * level - order_wide * order_wide, 1.0)
    )
    lower = jnp.sqrt(
        jnp.maximum((level - 1.0) * (level - 1.0) - order_wide * order_wide, 0.0)
        / jnp.maximum(4.0 * (level - 1.0) * (level - 1.0) - 1.0, 1.0)
    )
    upper, lower = (
        jnp.broadcast_to(lax.optimization_barrier(part)[:, :, None], part.shape + (LANES,))
        for part in (upper, lower)
    )
    places = jnp.arange(total).astype(jnp.int32)
    degrees = jnp.arange(degree_range).astype(jnp.int32)
    where = jnp.sum(
        jnp.where(degree_table[None, :] == degrees[:, None], places[None, :], 0), axis=1
    )
    where = jnp.minimum(where, total - 1).astype(jnp.int32)
    unroll = next(u for u in (8, 6, 5, 4, 3, 2, 1) if degree_range % u == 0)
    vmem = pl.BlockSpec(memory_space=pltpu.VMEM)
    return pl.pallas_call(
        functools.partial(recurrence_kernel, unroll),
        out_shape=jax.ShapeDtypeStruct((total, slots, latitude_count), jnp.bfloat16),
        in_specs=[pl.BlockSpec(memory_space=pltpu.SMEM)] + [vmem] * 5,
        out_specs=vmem,
        cost_estimate=pl.CostEstimate(
            flops=6 * degree_range * slots * latitude_count,
            bytes_accessed=24 * 1024 * 1024,
            transcendentals=0,
        ),
        name="legendre",
    )(
        where,
        upper,
        lower,
        jnp.broadcast_to(orders[:, None], (slots, LANES)),
        jnp.broadcast_to(cosine, (slots, latitude_count)),
        start,
    )


def quadrature(latitude_count):
    angles = jnp.pi * (jnp.arange(latitude_count).astype(jnp.float32) + 0.5) / latitude_count
    return jnp.pi / latitude_count * jnp.sin(angles)


def dense_exchange():
    def exchange(value):
        return lax.all_to_all(value, "order", split_axis=0, concat_axis=0, tiled=True)

    return exchange, exchange


def packed_exchange(capacity, leave, arrive):
    place = jnp.arange(capacity).astype(jnp.int32)[None, :, None, None]
    leave_matrix = (leave[:, None] == place).astype(jnp.bfloat16)
    arrive_matrix = (arrive[:, None] == place).astype(jnp.bfloat16)

    def route(value, packer, unpacker):
        packed = jnp.einsum(
            "tpks,tksc->tpc", packer, value, preferred_element_type=jnp.float32
        ).astype(jnp.bfloat16)
        moved = lax.all_to_all(packed, "order", split_axis=0, concat_axis=0, tiled=True)
        return jnp.einsum(
            "tpks,tpc->tksc", unpacker, moved, preferred_element_type=jnp.float32
        ).astype(jnp.bfloat16)

    return (
        lambda value: route(value, leave_matrix, arrive_matrix),
        lambda value: route(value, arrive_matrix, leave_matrix),
    )


def layer(exchanges, cotangent, stored_coefficients, weights, table, mine, degree_table, *ranks):
    return layer_body(
        exchanges(*ranks), cotangent, stored_coefficients, weights, table, mine, degree_table
    )


def layer_body(exchanges, cotangent, stored_coefficients, weights, table, mine, degree_table):
    send, back = exchanges
    slots, latitude_count, batch_size, parts, width = cotangent.shape
    degree_range = stored_coefficients.shape[1]
    rows = batch_size * parts
    cot = cotangent.reshape(slots, latitude_count, rows, width)
    stored = stored_coefficients.reshape(slots, degree_range, rows, width)
    degrees = jnp.arange(degree_range).astype(jnp.int32)
    pick = (degree_table[:, None, None] == degrees[None, None, :]) & (
        degrees[None, None, :] >= mine[None, :, None]
    )
    pick = pick.astype(jnp.bfloat16).reshape(table.shape[:3] + (degree_range,))

    def project(matrix, source):
        return jnp.einsum(
            "tksj,sjc->tksc", matrix, source, preferred_element_type=jnp.float32
        ).astype(jnp.bfloat16)

    gathered, saved, mixing, outputs = [], [], [], []
    for r in range(rows):
        adjoint = send(project(table, cot[:, :, r]))
        gathered.append(lax.all_gather(adjoint, "chan", axis=3, tiled=True))
    for r in range(rows):
        saved.append(send(project(pick, stored[:, :, r])))
    quad = quadrature(latitude_count)
    for r in range(rows):
        coefficient = jnp.einsum(
            "nksd,kcd->nksc", gathered[r], weights, preferred_element_type=jnp.float32
        ).astype(jnp.bfloat16)
        returned = back(coefficient)
        summed = jnp.einsum("tksj,tksc->sjc", table, returned, preferred_element_type=jnp.float32)
        outputs.append((summed * quad[None, :, None]).astype(jnp.bfloat16))
    for r in range(rows):
        mixing.append(
            jnp.einsum("nksc,nksd->kcd", saved[r], gathered[r], preferred_element_type=jnp.float32)
        )
    mixing_gradient = sum(mixing[1:], mixing[0]).astype(jnp.bfloat16)
    return jnp.stack(outputs, axis=2).reshape(cotangent.shape), mixing_gradient


def per_device(cotangent, stored_coefficients, weights, order_table, degree_table):
    slots, latitude_count = cotangent.shape[:2]
    degree_range = stored_coefficients.shape[1]
    peers = lax.axis_size("order")
    position = lax.axis_index("order")
    mine = lax.dynamic_slice_in_dim(order_table, position * slots, slots)
    owned = lax.dynamic_slice_in_dim(degree_table, position * slots, slots)
    table = picked_legendre(mine, degree_table, degree_range, latitude_count)
    table = table.reshape(peers, slots, slots, latitude_count)
    operands = (cotangent, stored_coefficients, weights, table, mine, degree_table)

    full = slots * slots
    live = degree_range * (degree_range + 1) / 2 / (peers * slots) ** 2
    spread = (full * (2 * slots + 1) / 12) ** 0.5
    capacity = -(-int(live * full + SPREADS * spread) // 16) * 16
    dense = functools.partial(layer, lambda *ranks: dense_exchange())
    if capacity > 0.85 * full:
        return dense(*operands)

    def places(orders, degree_rows):
        valid = (degree_rows >= orders) & (degree_rows < degree_range)
        flags = valid.reshape(-1, full).astype(jnp.bfloat16)
        index = jnp.arange(full)
        before = (index[:, None] < index[None, :]).astype(jnp.bfloat16)
        rank = jnp.dot(flags, before, preferred_element_type=jnp.float32).astype(jnp.int32)
        return jnp.where(valid, rank.reshape(valid.shape), -1)

    leave = places(mine[None, None, :], degree_table.reshape(peers, slots)[:, :, None])
    arrive = places(order_table.reshape(peers, slots)[:, None, :], owned[None, :, None])
    order_rows = order_table.reshape(peers, 1, slots, 1)
    degree_rows = degree_table.reshape(1, peers, 1, slots)
    counts = jnp.sum(
        ((degree_rows >= order_rows) & (degree_rows < degree_range)).astype(jnp.int32), axis=(2, 3)
    )
    fits = jnp.max(counts) <= capacity
    packed = functools.partial(layer, functools.partial(packed_exchange, capacity))
    return lax.cond(fits, packed, dense, *operands, leave, arrive)


def solution(mesh):
    return jax.shard_map(
        per_device,
        mesh=mesh,
        in_specs=(
            P("order", None, None, None, "chan"),
            P("order", None, None, None, "chan"),
            P("order", "chan", None),
            P(),
            P(),
        ),
        out_specs=(P("order", None, None, None, "chan"), P("order", "chan", None)),
        check_vma=False,
    )
```
